32 devices in a mesh: shard: 8 (over z, y), ctx: 2 (over x), tensor: 2 (over core).
Axes of the slice: x: 2, y: 2, z: 4, core: 2. Of those that a mesh axis runs over, the one named last changes fastest.
Arguments:
- tokens: bfloat16 [16384, 1536], P(('shard', 'ctx')), may hold values from -6 to 6
- segment_ids: int32 [8, 2048], P('shard'), may hold values from 0 to 7, never falling along the last dimension, each value on 1 to 1024 neighbouring positions
- norm_gain: bfloat16 [1536], P('shard'), may hold values from 0.099609375 to 1.8984375
- w_z: bfloat16 [1536, 3072], P('shard', 'tensor'), may hold values from -0.15625 to 0.15625
- w_x: bfloat16 [1536, 3072], P('shard', 'tensor'), may hold values from -0.15625 to 0.15625
- w_bc: bfloat16 [1536, 256], P('shard'), may hold values from -0.15625 to 0.15625
- w_dt: bfloat16 [1536, 48], P('shard', 'tensor'), may hold values from -0.15625 to 0.15625
- conv_x: bfloat16 [4, 48, 64], P(None, 'tensor', 'shard'), may hold values from -0.5 to 0.5
- conv_x_bias: bfloat16 [48, 64], P('tensor', 'shard'), may hold values from -0.5 to 0.5
- conv_bc: bfloat16 [4, 2, 128], P(None, None, 'shard'), may hold values from -0.5 to 0.5
- conv_bc_bias: bfloat16 [2, 128], P(None, 'shard'), may hold values from -0.5 to 0.5
- a_log: float32 [48], P('tensor'), may hold values from 0 to 2.5
- dt_bias: float32 [48], P('tensor'), may hold values from -8 to -2
- d_skip: float32 [48], P('tensor'), may hold values from 0.5 to 1.5
- gate_gain: bfloat16 [48, 64], P('tensor', 'shard'), may hold values from 0.099609375 to 1.8984375
- w_out: bfloat16 [3072, 1536], P('tensor', 'shard'), may hold values from -0.109375 to 0.109375
- cotangent: bfloat16 [16384, 1536], P(('shard', 'ctx'), 'tensor'), may hold values from -6 to 6
Outputs:
- block_out: bfloat16 [16384, 1536], P(('shard', 'ctx'), 'tensor')
- token_input_gradient: float32 [16384, 1536], P(('shard', 'ctx'), 'tensor')
- grad_norm_gain: float32 [1536], P('shard')
- grad_w_z: float32 [1536, 3072], P('shard', 'tensor')
- grad_w_x: float32 [1536, 3072], P('shard', 'tensor')
- grad_w_bc: float32 [1536, 256], P('shard')
- grad_w_dt: float32 [1536, 48], P('shard', 'tensor')
- grad_conv_x: float32 [4, 48, 64], P(None, 'tensor', 'shard')
- grad_conv_x_bias: float32 [48, 64], P('tensor', 'shard')
- grad_conv_bc: float32 [4, 2, 128], P(None, None, 'shard')
- grad_conv_bc_bias: float32 [2, 128], P(None, 'shard')
- grad_a_log: float32 [48], P('tensor')
- grad_dt_bias: float32 [48], P('tensor')
- grad_d_skip: float32 [48], P('tensor')
- grad_gate_gain: float32 [48, 64], P('tensor', 'shard')
- grad_w_out: float32 [3072, 1536], P('tensor', 'shard')
The draws below stay inside these ranges and needn't reach their ends.
Inputs may be any that keep to these rules, and one draw needn't show every extreme that they name: `segment_ids`: in each row (one sequence of 2048 tokens) the numbers never fall; every run of equal numbers (a document) has 1 to 1024 tokens, and some run has exactly 1024.
All inputs are finite; a program needn't handle non-finite values.
Results may differ from the reference program's by a relative error of at most 0.0084.
Values may be sent and summed in bfloat16 or wider, within the bound.
No kernel may reach another device: no remote copies, remote signals or barrier semaphores. Data moves between devices by JAX's collectives and lax.ppermute only.
A program may use at most 576 MiB of HBM per device.

```python
import math
import jax
import jax.numpy as jnp
import numpy as np
from jax import lax

D = 1536
HEADS = 48
HEADDIM = 64
NSTATE = 128
INNER = 3072
KCONV = 4
GROUP = 256
DOCS = 8
LENGTH = 2048
LONGEST = 1024
SEQS = 8
TOKENS = 16384


def steps_of(key, extent, split, low, largest):
    def one(axis_at, shards_of):
        heights = jax.random.uniform(jax.random.fold_in(jax.random.fold_in(key, 6), axis_at), (shards_of,), jnp.float32, low / len(split), largest / len(split))
        return jnp.repeat(jnp.exp(heights), extent[axis_at] // shards_of).reshape((-1,) + (1,) * (len(extent) - axis_at - 1))

    level = one(*split[0])
    for cut in split[1:]:
        level = level * one(*cut)
    return level


def length_profile(number_of, total, limit, slope):
    loads = [(1 << 20) // math.isqrt(grade ** slope) + 1 for grade in range(2, number_of + 1)]
    rest, given = total - limit - (number_of - 1), [1] * (number_of - 1)
    while rest > 0:
        movable = [i for i in range(number_of - 1) if given[i] < limit]
        whole, remaining = sum([loads[i] for i in movable]), rest
        for i in movable:
            extra = min(limit - given[i], max(1, remaining * loads[i] // whole), rest)
            given[i] = given[i] + extra
            rest = rest - extra
    return np.array([limit] + given)


def ragged_sizes(own_key, number_of, total, reach, slope):
    if number_of == 2:
        one = jax.random.randint(own_key, (), max(1, total - reach), min(reach, total - 1) + 1)
        return jnp.stack([one, total - one])
    tallies = jnp.asarray(length_profile(number_of, total, reach, slope), jnp.int32)
    pairs = (number_of - 1) // 2
    donor, sink = tallies[1:1 + 2 * pairs:2], tallies[2:2 + 2 * pairs:2]
    slack = jnp.minimum(donor - 1, reach - sink)
    passed = jax.random.randint(jax.random.fold_in(own_key, 1), (pairs,), 0, 1 << 20) % (slack + 1)
    tallies = tallies.at[1:1 + 2 * pairs:2].set(donor - passed).at[2:2 + 2 * pairs:2].set(sink + passed)
    return tallies[jax.random.permutation(jax.random.fold_in(own_key, 2), number_of)]


def normal_values(key, dims, scale, most, split=(), dtype=jnp.bfloat16):
    level = steps_of(key, dims, split, -0.22, 0.18) if split else 1.0
    values = jax.random.normal(key, dims, jnp.float32) * scale * level
    return jnp.minimum(jnp.maximum(values, -most), most).astype(dtype)


def setup_inputs(seed: int = 0) -> dict:
    key_of = jax.random.split(jax.random.key(seed), 18)
    tokens = normal_values(key_of[0], (TOKENS, D), 1.0, 6.0, ((0, 16),))
    segment_ids = jax.vmap(lambda own: jnp.searchsorted(jnp.cumsum(ragged_sizes(own, DOCS, LENGTH, LONGEST, 0)), jnp.arange(LENGTH), side="right"))(jax.random.split(key_of[1], SEQS)).reshape((SEQS, LENGTH)).astype(jnp.int32)
    norm_gain = jnp.clip(1.0 + 0.18 * jax.random.normal(key_of[2], (D,), jnp.float32), 0.099609375, 1.8984375).astype(jnp.bfloat16)
    w_z = normal_values(key_of[3], (D, INNER), D ** -0.5, 0.15625, ((0, 8), (1, 2)))
    w_x = normal_values(key_of[4], (D, INNER), D ** -0.5, 0.15625, ((0, 8), (1, 2)))
    w_bc = normal_values(key_of[5], (D, 2 * NSTATE), D ** -0.5, 0.15625, ((0, 8),))
    w_dt = normal_values(key_of[6], (D, HEADS), D ** -0.5, 0.15625, ((0, 8), (1, 2)))
    conv_x = jnp.clip(jax.random.uniform(key_of[7], (KCONV, HEADS, HEADDIM), jnp.float32, -0.5, 0.5) * steps_of(key_of[7], (KCONV, HEADS, HEADDIM), ((1, 2), (2, 8)), -0.4, 0.0), -0.5, 0.5).astype(jnp.bfloat16)
    conv_x_bias = jnp.clip(jax.random.uniform(key_of[8], (HEADS, HEADDIM), jnp.float32, -0.5, 0.5) * steps_of(key_of[8], (HEADS, HEADDIM), ((0, 2), (1, 8)), -0.4, 0.0), -0.5, 0.5).astype(jnp.bfloat16)
    conv_bc = jnp.clip(jax.random.uniform(key_of[9], (KCONV, 2, NSTATE), jnp.float32, -0.5, 0.5) * steps_of(key_of[9], (KCONV, 2, NSTATE), ((2, 8),), -0.4, 0.0), -0.5, 0.5).astype(jnp.bfloat16)
    conv_bc_bias = jnp.clip(jax.random.uniform(key_of[10], (2, NSTATE), jnp.float32, -0.5, 0.5) * steps_of(key_of[10], (2, NSTATE), ((1, 8),), -0.4, 0.0), -0.5, 0.5).astype(jnp.bfloat16)
    a_log = jnp.clip(2.5 * jax.random.uniform(key_of[11], (HEADS,), jnp.float32) ** steps_of(key_of[11], (HEADS,), ((0, 2),), -0.2, 0.2), 0.0, 2.5)
    dt_bias = jnp.clip(-8.0 + 6.0 * jax.random.uniform(key_of[12], (HEADS,), jnp.float32) ** steps_of(key_of[12], (HEADS,), ((0, 2),), -0.2, 0.2), -8.0, -2.0)
    d_skip = jnp.clip(0.5 + 1.0 * jax.random.uniform(key_of[13], (HEADS,), jnp.float32) ** steps_of(key_of[13], (HEADS,), ((0, 2),), -0.2, 0.2), 0.5, 1.5)
    gate_gain = jnp.clip(1.0 + 0.18 * jax.random.normal(key_of[14], (HEADS, HEADDIM), jnp.float32), 0.099609375, 1.8984375).astype(jnp.bfloat16)
    w_out = normal_values(key_of[15], (INNER, D), INNER ** -0.5, 0.109375, ((0, 2), (1, 8)))
    cotangent = normal_values(key_of[16], (TOKENS, D), 1.0, 6.0, ((0, 16), (1, 2)))
    return {"tokens": tokens, "segment_ids": segment_ids, "norm_gain": norm_gain, "w_z": w_z, "w_x": w_x, "w_bc": w_bc, "w_dt": w_dt, "conv_x": conv_x, "conv_x_bias": conv_x_bias, "conv_bc": conv_bc, "conv_bc_bias": conv_bc_bias, "a_log": a_log, "dt_bias": dt_bias, "d_skip": d_skip, "gate_gain": gate_gain, "w_out": w_out, "cotangent": cotangent}


EPSILON = 1e-05
HIGHEST = lax.Precision.HIGHEST

def convolve(extended, seg_ext, conv_weight, conv_bias):
    tap_count = conv_weight.shape[0]
    row_count = extended.shape[0] - tap_count + 1
    own_segs = seg_ext[tap_count - 1:]
    summed = jnp.broadcast_to(conv_bias[None, :], (row_count, conv_bias.shape[0]))
    for offset in range(tap_count):
        same_doc = (seg_ext[offset:offset + row_count] == own_segs).astype(jnp.float32)
        summed = summed + conv_weight[offset][None, :] * extended[offset:offset + row_count] * same_doc[:, None]
    return jax.nn.silu(summed)

def ssd_scan(mixer_x, b_mat, c_mat, dt_raw, dt_bias, a_log, d_skip, segments, seg_prev, state_in, group):
    row_count = mixer_x.shape[0]
    head_count = state_in.shape[0]
    head_width = state_in.shape[1]
    state_width = state_in.shape[2]
    block_count = row_count // group
    step_size = jax.nn.softplus(dt_raw + dt_bias[None, :])
    log_decay = -step_size * jnp.exp(a_log)[None, :]
    before = jnp.concatenate([jnp.reshape(seg_prev, (1,)), segments[:-1]])
    causal = jnp.arange(group)[:, None] >= jnp.arange(group)[None, :]

    def advance(carry_state, block_in):
        x_blk, b_blk, c_blk, s_blk, r_blk, g_blk, p_blk = block_in
        x_heads = x_blk.reshape(group, head_count, head_width)
        cumulative = jnp.cumsum(r_blk, axis=0)
        inside = (g_blk[:, None] == g_blk[None, :]) & causal
        spread = cumulative.T[:, :, None] - cumulative.T[:, None, :]
        decay_mat = jnp.where(inside[None], jnp.exp(jnp.where(inside[None], spread, 0.0)), 0.0)
        scores = jnp.dot(c_blk, b_blk.T, precision=HIGHEST)
        mixing = decay_mat * scores[None] * s_blk.T[:, None, :]
        output = jnp.einsum('hts,shp->thp', mixing, x_heads, precision=HIGHEST)
        enter_gate = jnp.where((g_blk == p_blk[0])[:, None], jnp.exp(cumulative), 0.0)
        carried = jnp.einsum('tn,hpn->thp', c_blk, carry_state, precision=HIGHEST)
        output = output + carried * enter_gate[:, :, None] + d_skip[None, :, None] * x_heads
        last_sum = cumulative[-1]
        tail_gate = jnp.where((g_blk == g_blk[-1])[:, None], jnp.exp(last_sum[None, :] - cumulative), 0.0) * s_blk
        keep_gate = jnp.where(g_blk[-1] == p_blk[0], jnp.exp(last_sum), 0.0)
        carry_state = keep_gate[:, None, None] * carry_state + jnp.einsum('shp,sn->hpn', x_heads * tail_gate[:, :, None], b_blk, precision=HIGHEST)
        return (carry_state, output.reshape(group, head_count * head_width))
    blocks = (mixer_x.reshape(block_count, group, head_count * head_width), b_mat.reshape(block_count, group, state_width), c_mat.reshape(block_count, group, state_width), step_size.reshape(block_count, group, head_count), log_decay.reshape(block_count, group, head_count), segments.reshape(block_count, group), before.reshape(block_count, group))
    state_end, outputs = lax.scan(advance, state_in, blocks)
    return (outputs.reshape(row_count, head_count * head_width), state_end)

def sequence_pass(tokens, segments, cotangent, params):
    norm_gain, w_z, w_x, w_bc, w_dt, conv_x, conv_x_bias, conv_bc, conv_bc_bias, a_log, dt_bias, d_skip, gate_gain, w_out = params
    inner = w_z.shape[1]
    state_width = w_bc.shape[1] // 2
    head_count = a_log.shape[0]
    head_width = inner // head_count
    tap_count = conv_x.shape[0]
    channels = inner + 2 * state_width
    tokens_f = tokens.astype(jnp.float32)
    inverse_deviation_input = lax.rsqrt(lax.optimization_barrier(jnp.mean(tokens_f * tokens_f, axis=1, keepdims=True)) + EPSILON)
    standardized_input = tokens_f * inverse_deviation_input
    input_gain_weight = norm_gain.astype(jnp.float32)[None, :]
    normed = (standardized_input * input_gain_weight).astype(jnp.bfloat16)
    z_pre = jnp.dot(normed, w_z, preferred_element_type=jnp.float32)
    x_pre = jnp.dot(normed, w_x, preferred_element_type=jnp.float32)
    bc_pre = jnp.dot(normed, w_bc, preferred_element_type=jnp.float32)
    dt_pre = jnp.dot(normed, w_dt, preferred_element_type=jnp.float32)
    conv_weight = jnp.concatenate([conv_x.reshape(tap_count, inner), conv_bc.reshape(tap_count, 2 * state_width)], axis=1).astype(jnp.float32)
    conv_bias = jnp.concatenate([conv_x_bias.reshape(inner), conv_bc_bias.reshape(2 * state_width)]).astype(jnp.float32)
    extended = jnp.concatenate([jnp.zeros((tap_count - 1, channels), jnp.float32), jnp.concatenate([x_pre, bc_pre], axis=1)], axis=0)
    seg_ext = jnp.concatenate([jnp.full((tap_count - 1,), -1, jnp.int32), segments])
    seg_prev = jnp.array(-1, jnp.int32)
    zero_state = jnp.zeros((head_count, head_width, state_width), jnp.float32)

    def conv_part(ext_in, weight_in, bias_in):
        return convolve(ext_in, seg_ext, weight_in, bias_in)
    activated, conv_back = jax.vjp(conv_part, extended, conv_weight, conv_bias)
    mixer_x = activated[:, :inner]
    b_mat = activated[:, inner:inner + state_width]
    c_mat = activated[:, inner + state_width:]

    def ssd_part(mixer_in, b_input, c_input, rate_raw, bias_rate, log_rates, skip_gain):
        return ssd_scan(mixer_in, b_input, c_input, rate_raw, bias_rate, log_rates, skip_gain, segments, seg_prev, zero_state, GROUP)[0]
    mixed, ssd_back = jax.vjp(ssd_part, mixer_x, b_mat, c_mat, dt_pre, dt_bias, a_log, d_skip)
    sigmoid_z = jax.nn.sigmoid(z_pre)
    gate_act = z_pre * sigmoid_z
    gated = mixed * gate_act
    rstd_gate = lax.rsqrt(lax.optimization_barrier(jnp.mean(gated * gated, axis=1, keepdims=True)) + EPSILON)
    gated_hat = gated * rstd_gate
    gain_gate = gate_gain.reshape(inner).astype(jnp.float32)[None, :]
    gated_out = (gated_hat * gain_gate).astype(jnp.bfloat16)
    branch = jnp.dot(gated_out, w_out, preferred_element_type=jnp.float32)
    block_out = (tokens_f + branch).astype(jnp.bfloat16)
    grad_w_out = lax.dot_general(gated_out, cotangent, (((0,), (0,)), ((), ())), preferred_element_type=jnp.float32)
    d_out = lax.dot_general(cotangent, w_out, (((1,), (1,)), ((), ())), preferred_element_type=jnp.float32)
    grad_gate = lax.optimization_barrier(jnp.sum(d_out * gated_hat, axis=0))
    d_hat = d_out * gain_gate
    d_gated = rstd_gate * (d_hat - gated_hat * lax.optimization_barrier(jnp.mean(d_hat * gated_hat, axis=1, keepdims=True)))
    d_mixed = d_gated * gate_act
    d_z = d_gated * mixed * sigmoid_z * (1.0 + z_pre * (1.0 - sigmoid_z))
    d_mixer, d_bmat, d_cmat, d_rate, d_bias_dt, d_alog, d_dskip = ssd_back(d_mixed)
    d_ext, d_convw, d_convb = conv_back(jnp.concatenate([d_mixer, d_bmat, d_cmat], axis=1))
    d_input = d_ext[tap_count - 1:]
    z_grad16 = d_z.astype(jnp.bfloat16)
    x_grad16 = d_input[:, :inner].astype(jnp.bfloat16)
    bc_grad16 = d_input[:, inner:].astype(jnp.bfloat16)
    dt_grad16 = d_rate.astype(jnp.bfloat16)

    def weight_grad(grad16):
        return lax.dot_general(normed, grad16, (((0,), (0,)), ((), ())), preferred_element_type=jnp.float32)

    def input_grad(grad16, weight):
        return lax.dot_general(grad16, weight, (((1,), (1,)), ((), ())), preferred_element_type=jnp.float32)
    normalized_gradient = input_grad(z_grad16, w_z) + input_grad(x_grad16, w_x) + input_grad(bc_grad16, w_bc) + input_grad(dt_grad16, w_dt)
    centered_input_gradient = normalized_gradient * input_gain_weight
    grad_norm = lax.optimization_barrier(jnp.sum(normalized_gradient * standardized_input, axis=0))
    token_input_gradient = inverse_deviation_input * (centered_input_gradient - standardized_input * lax.optimization_barrier(jnp.mean(centered_input_gradient * standardized_input, axis=1, keepdims=True))) + cotangent.astype(jnp.float32)
    grads_seq = (grad_norm, weight_grad(z_grad16), weight_grad(x_grad16), weight_grad(bc_grad16), weight_grad(dt_grad16), d_convw[:, :inner].reshape(tap_count, head_count, head_width), d_convb[:inner].reshape(head_count, head_width), d_convw[:, inner:].reshape(tap_count, 2, state_width), d_convb[inner:].reshape(2, state_width), d_alog, d_bias_dt, d_dskip, grad_gate.reshape(head_count, head_width), grad_w_out)
    return (block_out, token_input_gradient, grads_seq)

def reference(tokens, segment_ids, norm_gain, w_z, w_x, w_bc, w_dt, conv_x, conv_x_bias, conv_bc, conv_bc_bias, a_log, dt_bias, d_skip, gate_gain, w_out, cotangent):
    seq_count = segment_ids.shape[0]
    seq_len = segment_ids.shape[1]
    model = tokens.shape[1]
    params = (norm_gain, w_z, w_x, w_bc, w_dt, conv_x, conv_x_bias, conv_bc, conv_bc_bias, a_log, dt_bias, d_skip, gate_gain, w_out)
    token_seqs = tokens.reshape(seq_count, seq_len, model)
    cot_seqs = cotangent.reshape(seq_count, seq_len, model)
    initial = jax.tree.map(lambda param: jnp.zeros(param.shape, jnp.float32), params)

    def one_sequence(running, item_in):
        tok_in, seg_in, cot_in = item_in
        out_seq, dx_seq, grads_seq = sequence_pass(tok_in, seg_in, cot_in, params)
        running = jax.tree.map(lambda left, right: left + right, running, grads_seq)
        return (running, (out_seq, dx_seq))
    totals, stacked = lax.scan(one_sequence, initial, (token_seqs, segment_ids, cot_seqs))
    outs_all = stacked[0].reshape(seq_count * seq_len, model)
    dx_all = stacked[1].reshape(seq_count * seq_len, model)
    return (outs_all, dx_all, totals[0], totals[1], totals[2], totals[3], totals[4], totals[5], totals[6], totals[7], totals[8], totals[9], totals[10], totals[11], totals[12], totals[13])
```

```python
import functools
import math
import jax
import jax.numpy as jnp
from jax import lax
from jax.experimental import pallas as pl
from jax.experimental.pallas import tpu as pltpu
from jax.sharding import PartitionSpec as P

BF, F32 = jnp.bfloat16, jnp.float32
CHUNK = 128
LANES = 128
LOG2E = math.log2(math.e)
EPSILON = 1e-05


def dot(a, b, ca, cb):
    return lax.dot_general(a, b, (((ca,), (cb,)), ((), ())), preferred_element_type=F32)


def halves(v):
    high = v.astype(BF)
    return high, (v - high.astype(F32)).astype(BF)


def sigmoid(v):
    return 1.0 / (1.0 + jnp.exp(-v))


def softplus(v):
    return jnp.maximum(v, 0.0) + jnp.log(1.0 + jnp.exp(-jnp.abs(v)))


def lane_spread(cols, first, count, width):
    lane = lax.broadcasted_iota(jnp.int32, (1, LANES), 1)
    out = cols[:, first : first + 1]
    for j in range(1, count):
        out = jnp.where(lane >= j * width, cols[:, first + j : first + j + 1], out)
    return jnp.broadcast_to(out, (cols.shape[0], LANES))


def head_masks(count, width):
    lane = lax.broadcasted_iota(jnp.int32, (1, LANES), 1)
    return [
        jnp.where((lane >= j * width) & (lane < (j + 1) * width), 1.0, 0.0).astype(BF)
        for j in range(count)
    ]


def rates(raw, headp, seg_col, seg_row):
    L = raw.shape[0]
    row_at = lax.broadcasted_iota(jnp.int32, (L, L), 0)
    col_at = lax.broadcasted_iota(jnp.int32, (L, L), 1)
    same = seg_col == seg_row
    step = softplus(raw + headp[0:1])
    decay = step * headp[1:2]
    before = jnp.where(same & (row_at >= col_at), 1.0, 0.0).astype(BF)
    hi, lo = halves(decay)
    total = (dot(before, hi, 1, 0) + dot(before, lo, 1, 0)) * LOG2E
    return step, decay, total, same, row_at, col_at


def fwd_kernel(width, u_ref, cols_ref, rows_ref, conv_ref, headp_ref, lanep_ref,
               y_ref, pre_ref, hin_ref, state, ubuf):
    L = CHUNK
    inner = y_ref.shape[1]
    per = LANES // width
    tiles = inner // LANES
    at = pl.program_id(0)

    @pl.when(at == 0)
    def _():
        state[...] = jnp.zeros_like(state)
        ubuf[0:8] = jnp.zeros((8, ubuf.shape[1]), F32)

    @pl.when(at > 0)
    def _():
        ubuf[0:8] = ubuf[L : L + 8]

    channels = ubuf.shape[1]
    acts = []
    cols = cols_ref[...]
    for i in range(channels // LANES):
        sl = slice(i * LANES, (i + 1) * LANES)
        cur = u_ref[:, sl]
        ubuf[8 : 8 + L, sl] = cur
        pre = conv_ref[4:5, sl] + conv_ref[3:4, sl] * cur
        for k in range(1, 4):
            pre = pre + (conv_ref[3 - k : 4 - k, sl] * ubuf[8 - k : 8 - k + L, sl]) * cols[:, k : k + 1]
        pre_ref[:, sl] = pre
        acts.append(pre * sigmoid(pre))
    b_act = acts[tiles].astype(BF)
    c_act = acts[tiles + 1].astype(BF)
    seg_row = rows_ref[0][0:1]
    step, decay, total, same, row_at, col_at = rates(
        u_ref[:, channels : channels + LANES], headp_ref[...], cols[:, 0:1], seg_row
    )
    bias = jnp.where(same & (row_at >= col_at), 0.0, -1e30)
    total_t = jnp.transpose(total)
    scores = dot(c_act, b_act, 1, 1)
    last = total[L - 1 : L]
    enter = cols[:, 7:8] * jnp.exp2(total)
    tail = cols[:, 8:9] * jnp.exp2(jnp.minimum(last - total, 0.0))
    keep = cols[L - 1 : L, 7:8] * jnp.exp2(last)
    masks = head_masks(per, width)
    h_low = state[...].astype(BF)
    hin_ref[0] = h_low
    carried = dot(c_act, h_low, 1, 0)
    pushed = []
    for i in range(tiles):
        sl = slice(i * LANES, (i + 1) * LANES)
        x = acts[i]
        scaled = (x * lane_spread(step, i * per, per, width)).astype(BF)
        mix = [
            (jnp.exp2(total[:, h : h + 1] - total_t[h : h + 1] + bias) * scores).astype(BF)
            for h in range(i * per, (i + 1) * per)
        ]
        out = dot(
            jnp.concatenate(mix, axis=1),
            jnp.concatenate([scaled * m for m in masks], axis=0), 1, 0)
        out = out + carried[:, sl] * lane_spread(enter, i * per, per, width)
        y_ref[:, sl] = out + lanep_ref[0:1, sl] * x
        pushed.append((scaled.astype(F32) * lane_spread(tail, i * per, per, width)).astype(BF))
    grown = dot(b_act, jnp.concatenate(pushed, axis=1), 0, 0)
    for i in range(tiles):
        sl = slice(i * LANES, (i + 1) * LANES)
        state[:, sl] = state[:, sl] * lane_spread(keep, i * per, per, width) + grown[:, sl]


def ssd_forward(u, cols, rows, convp, headp, lanep, width):
    count = u.shape[0]
    inner = lanep.shape[1]
    channels = convp.shape[1]
    nstate = (channels - inner) // 2
    n = count // CHUNK
    whole = lambda a: pl.BlockSpec(a.shape, lambda i: (0,) * a.ndim)
    rowblk = lambda c: pl.BlockSpec((CHUNK, c), lambda i: (i, 0))
    return pl.pallas_call(
        functools.partial(fwd_kernel, width),
        grid=(n,),
        in_specs=[rowblk(u.shape[1]), rowblk(cols.shape[1]),
                  pl.BlockSpec((1,) + rows.shape[1:], lambda i: (i, 0, 0)),
                  whole(convp), whole(headp), whole(lanep)],
        out_specs=[rowblk(inner), rowblk(channels),
                   pl.BlockSpec((1, nstate, inner), lambda i: (i, 0, 0))],
        out_shape=[jax.ShapeDtypeStruct((count, inner), F32),
                   jax.ShapeDtypeStruct((count, channels), F32),
                   jax.ShapeDtypeStruct((n, nstate, inner), BF)],
        scratch_shapes=[pltpu.VMEM((nstate, inner), F32), pltpu.VMEM((CHUNK + 8, channels), F32)],
        name="ssd_forward",
    )(u, cols, rows, convp, headp, lanep)


def bwd_kernel(width, dy_ref, y_ref, u_ref, pre_ref, hin_ref, cols_ref, rows_ref, conv_ref,
               headp_ref, lanep_ref, pick_ref,
               dx_ref, dbc_ref, ddt_ref, gconv_ref, ghead_ref, gskip_ref,
               dstate, dbuf, inner_hi):
    L = CHUNK
    inner = dx_ref.shape[1]
    per = LANES // width
    tiles = inner // LANES
    at = pl.program_id(0)

    @pl.when(at == 0)
    def _():
        dstate[...] = jnp.zeros_like(dstate)
        dbuf[L : L + 8] = jnp.zeros((8, inner), F32)
        gconv_ref[...] = jnp.zeros_like(gconv_ref)
        ghead_ref[...] = jnp.zeros_like(ghead_ref)
        gskip_ref[...] = jnp.zeros_like(gskip_ref)

    @pl.when(at > 0)
    def _():
        dbuf[L : L + 8] = dbuf[0:8]

    channels = pre_ref.shape[1]
    cols = cols_ref[...]
    seg_row = rows_ref[0][0:1]
    raw = u_ref[:, channels : channels + LANES]
    step, decay, total, same, row_at, col_at = rates(raw, headp_ref[...], cols[:, 0:1], seg_row)
    after = same & (row_at <= col_at)
    bias = jnp.where(after, 0.0, -1e30)
    total_t = jnp.transpose(total)
    last = total[L - 1 : L]
    enter = cols[:, 7:8] * jnp.exp2(total)
    tail = cols[:, 8:9] * jnp.exp2(jnp.minimum(last - total, 0.0))
    keep = cols[L - 1 : L, 7:8] * jnp.exp2(last)
    masks = head_masks(per, width)

    def act(i):
        pre = pre_ref[:, i * LANES : (i + 1) * LANES]
        sig = sigmoid(pre)
        return pre * sig, sig * (1.0 + pre * (1.0 - sig))

    b_act = act(tiles)[0].astype(BF)
    c_act = act(tiles + 1)[0].astype(BF)
    scores_t = dot(b_act, c_act, 1, 1)
    dh = dstate[...]
    dh_low = dh.astype(BF)
    h_low = hin_ref[0]
    from_state = dot(b_act, dh_low, 1, 0)
    d_scores = jnp.zeros((L, L), F32)
    entered, pushed = [], []
    last_parts = []
    for i in range(tiles):
        sl = slice(i * LANES, (i + 1) * LANES)
        x, slope = act(i)
        step_l = lane_spread(step, i * per, per, width)
        scaled = (x * step_l).astype(BF)
        scaled_f = scaled.astype(F32)
        dy = dy_ref[:, sl]
        dy_f = dy.astype(F32)
        decays = [
            jnp.exp2(total_t[h : h + 1] - total[:, h : h + 1] + bias)
            for h in range(i * per, (i + 1) * per)
        ]
        mix = jnp.concatenate([(d * scores_t).astype(BF) for d in decays], axis=1)
        dxs = dot(mix, jnp.concatenate([dy * m for m in masks], axis=0), 1, 0)
        tail_l = lane_spread(tail, i * per, per, width)
        dxt = from_state[:, sl] * tail_l
        dxs = dxs + dxt
        d_mix = dot(jnp.concatenate([scaled * m for m in masks], axis=0), dy, 1, 1)
        for j in range(per):
            d_scores = d_scores + d_mix[j * L : (j + 1) * L] * decays[j]
        skip = lanep_ref[0:1, sl]
        grow = dy_f * (y_ref[:, sl] - skip * x) - scaled_f * dxs
        direct = x * dxs
        for place, value in ((0, grow), (2, direct)):
            hi, lo = halves(value)
            inner_hi[:, place * inner + i * LANES : place * inner + (i + 1) * LANES] = hi
            inner_hi[:, (place + 1) * inner + i * LANES : (place + 1) * inner + (i + 1) * LANES] = lo
        gskip_ref[0:1, sl] += jnp.sum(dy_f * x, axis=0, keepdims=True)
        dyg = (dy_f * lane_spread(enter, i * per, per, width)).astype(BF)
        entered.append(dyg)
        pushed.append((scaled_f * tail_l).astype(BF))
        last_parts.append(
            jnp.sum(scaled_f * dxt, axis=0, keepdims=True)
            + jnp.sum(h_low[:, sl].astype(F32) * dh[:, sl], axis=0, keepdims=True)
            * lane_spread(keep, i * per, per, width)
        )
        dpre = (step_l * dxs + skip * dy_f) * slope
        dbuf[0:L, sl] = dpre
        u = u_ref[:, sl]
        du = conv_ref[3:4, sl] * dpre
        gconv_ref[4:5, sl] += jnp.sum(dpre, axis=0, keepdims=True)
        gconv_ref[3:4, sl] += jnp.sum(dpre * u, axis=0, keepdims=True)
        for k in range(1, 4):
            moved = dbuf[k : k + L, sl] * cols[:, 3 + k : 4 + k]
            du = du + conv_ref[3 - k : 4 - k, sl] * moved
            gconv_ref[3 - k : 4 - k, sl] += jnp.sum(moved * u, axis=0, keepdims=True)
        dx_ref[:, sl] = du.astype(BF)
    entered = jnp.concatenate(entered, axis=1)
    pushed = jnp.concatenate(pushed, axis=1)
    d_scores = d_scores.astype(BF)
    nst = b_act.shape[1]
    dbc_ref[:, 0:nst] = (dot(d_scores, c_act, 1, 0) + dot(pushed, dh_low, 1, 1)).astype(BF)
    dbc_ref[:, nst : 2 * nst] = (dot(d_scores, b_act, 0, 0) + dot(entered, h_low, 1, 1)).astype(BF)
    grown = dot(c_act, entered, 0, 0)
    for i in range(tiles):
        sl = slice(i * LANES, (i + 1) * LANES)
        dstate[:, sl] = dh[:, sl] * lane_spread(keep, i * per, per, width) + grown[:, sl]
    pick = pick_ref[...]
    d_total = dot(inner_hi[:, 0 : 2 * inner], pick, 1, 0)
    d_direct = dot(inner_hi[:, 2 * inner : 4 * inner], pick, 1, 0)
    lasts = jnp.broadcast_to(jnp.concatenate(last_parts, axis=1), (8, inner))
    hi, lo = halves(lasts)
    d_last = dot(jnp.concatenate([hi, lo], axis=1), pick, 1, 0)[0:1]
    hi, lo = halves(d_total)
    later = jnp.where(after, 1.0, 0.0).astype(BF)
    d_decay = dot(later, hi, 1, 0) + dot(later, lo, 1, 0) + cols[:, 8:9] * d_last
    d_step = d_direct + d_decay * headp_ref[1:2]
    d_raw = d_step * sigmoid(raw + headp_ref[0:1])
    ddt_ref[...] = d_raw.astype(BF)
    ghead_ref[0:1] += jnp.sum(d_decay * decay, axis=0, keepdims=True)
    ghead_ref[1:2] += jnp.sum(d_raw, axis=0, keepdims=True)


def ssd_backward(dy, y, u, pre, h_in, cols, rows, convp, headp, lanep, pick, width):
    count, inner = y.shape
    channels = convp.shape[1]
    nstate = (channels - inner) // 2
    n = count // CHUNK
    whole = lambda a: pl.BlockSpec(a.shape, lambda i: (0,) * a.ndim)
    rowblk = lambda c: pl.BlockSpec((CHUNK, c), lambda i: (n - 1 - i, 0))
    blk3 = lambda a: pl.BlockSpec((1,) + a.shape[1:], lambda i: (n - 1 - i, 0, 0))
    fixed = lambda s: pl.BlockSpec(s, lambda i: (0, 0))
    return pl.pallas_call(
        functools.partial(bwd_kernel, width),
        grid=(n,),
        in_specs=[rowblk(inner), rowblk(inner), rowblk(u.shape[1]), rowblk(channels), blk3(h_in),
                  rowblk(cols.shape[1]), blk3(rows), whole(convp), whole(headp), whole(lanep), whole(pick)],
        out_specs=[rowblk(inner), rowblk(2 * nstate), rowblk(LANES),
                   fixed((8, inner)), fixed((8, LANES)), fixed((8, inner))],
        out_shape=[jax.ShapeDtypeStruct((count, inner), BF),
                   jax.ShapeDtypeStruct((count, 2 * nstate), BF),
                   jax.ShapeDtypeStruct((count, LANES), BF),
                   jax.ShapeDtypeStruct((8, inner), F32),
                   jax.ShapeDtypeStruct((8, LANES), F32),
                   jax.ShapeDtypeStruct((8, inner), F32)],
        scratch_shapes=[pltpu.VMEM((nstate, inner), F32), pltpu.VMEM((CHUNK + 8, inner), F32),
                        pltpu.VMEM((CHUNK, 4 * inner), BF)],
        name="ssd_backward",
    )(dy, y, u, pre, h_in, cols, rows, convp, headp, lanep, pick)


def segment_tables(seg, chunk):
    count = seg.shape[0]
    n = count // chunk
    none = jnp.full((3,), -1, seg.dtype)
    padded = jnp.concatenate([none, seg, none])
    back = [padded[3 - k : 3 - k + count] == seg for k in range(1, 4)]
    ahead = [padded[3 + k : 3 + k + count] == seg for k in range(1, 4)]
    by = seg.reshape(n, chunk)
    prev = jnp.concatenate([none[:1], by[:-1, -1]])[:, None]
    enter = (by == prev).reshape(count)
    tail = (by == by[:, -1:]).reshape(count)
    table = [seg] + back + ahead + [enter, tail]
    table = jnp.stack([t.astype(F32) for t in table] + [jnp.zeros((count,), F32)] * (16 - len(table)), axis=1)
    rows = jnp.broadcast_to(by.astype(F32)[:, None, :], (n, 8, chunk))
    return table, rows


def head_pick(heads, width):
    lane = lax.broadcasted_iota(jnp.int32, (heads * width, LANES), 0) // width
    head = lax.broadcasted_iota(jnp.int32, (heads * width, LANES), 1)
    one = (lane == head).astype(BF)
    return jnp.concatenate([one, one], axis=0)


def stats_kernel(y_ref, z_ref, dout_ref, lanep_ref, out_ref):
    z = z_ref[...]
    gated = y_ref[...] * (z * sigmoid(z))
    cross = dout_ref[...] * lanep_ref[1:2] * gated
    ones = jnp.ones((8, gated.shape[1]), BF)

    def row(v):
        hi, lo = halves(v)
        return (dot(ones, hi, 1, 1) + dot(ones, lo, 1, 1))[0:1]

    out_ref[0] = jnp.concatenate([row(gated * gated), row(cross)], axis=0)


def gate_stats(y, z, dout, lanep):
    count, inner = y.shape
    n = count // CHUNK
    blk = pl.BlockSpec((CHUNK, inner), lambda i: (i, 0))
    return pl.pallas_call(
        stats_kernel,
        grid=(n,),
        in_specs=[blk, blk, blk, pl.BlockSpec(lanep.shape, lambda i: (0, 0))],
        out_specs=pl.BlockSpec((1, 2, CHUNK), lambda i: (i, 0, 0)),
        out_shape=jax.ShapeDtypeStruct((n, 2, CHUNK), F32),
        cost_estimate=pl.CostEstimate(
            flops=20 * count * inner, bytes_accessed=12 * count * inner, transcendentals=count * inner),
        name="gate_stats",
    )(y, z, dout, lanep)


def gate_kernel(inner_all, y_ref, z_ref, dout_ref, stats_ref, lanep_ref,
                out_ref, dz_ref, dy_ref, gain_ref):
    @pl.when(pl.program_id(0) == 0)
    def _():
        gain_ref[...] = jnp.zeros_like(gain_ref)

    stats = stats_ref[0]

    def column(row):
        return jnp.transpose(jnp.broadcast_to(row, (CHUNK, CHUNK)))

    rstd = lax.rsqrt(column(stats[0:1]) / inner_all + EPSILON)
    mean = column(stats[1:2]) * rstd / inner_all
    for i in range(out_ref.shape[1] // LANES):
        sl = slice(i * LANES, (i + 1) * LANES)
        y = y_ref[:, sl]
        z = z_ref[:, sl]
        dout = dout_ref[:, sl]
        gain = lanep_ref[1:2, sl]
        sig = sigmoid(z)
        silu = z * sig
        hat = y * silu * rstd
        d_gated = rstd * (dout * gain - hat * mean)
        out_ref[:, sl] = (hat * gain).astype(BF)
        dy_ref[:, sl] = (d_gated * silu).astype(BF)
        dz_ref[:, sl] = (d_gated * y * sig * (1.0 + z * (1.0 - sig))).astype(BF)
        gain_ref[0:1, sl] += jnp.sum(dout * hat, axis=0, keepdims=True)


def gate_backward(y, z, dout, stats, lanep, inner_all):
    count, inner = y.shape
    n = count // CHUNK
    blk = pl.BlockSpec((CHUNK, inner), lambda i: (i, 0))
    low = jax.ShapeDtypeStruct((count, inner), BF)
    return pl.pallas_call(
        functools.partial(gate_kernel, inner_all),
        grid=(n,),
        in_specs=[blk, blk, blk, pl.BlockSpec((1, 2, CHUNK), lambda i: (i, 0, 0)),
                  pl.BlockSpec(lanep.shape, lambda i: (0, 0))],
        out_specs=[blk, blk, blk, pl.BlockSpec((8, inner), lambda i: (0, 0))],
        out_shape=[low, low, low, jax.ShapeDtypeStruct((8, inner), F32)],
        cost_estimate=pl.CostEstimate(
            flops=30 * count * inner, bytes_accessed=18 * count * inner, transcendentals=count * inner),
        name="gate_backward",
    )(y, z, dout, stats, lanep)


def swap(v, axis, bit=1):
    count = lax.axis_size(axis)
    return lax.ppermute(v, axis, [(i, i ^ bit) for i in range(count)])


def gather_small(v, axis):
    count = lax.axis_size(axis)
    me = lax.axis_index(axis)
    out = v[None]
    bit = 1
    while bit < count:
        other = swap(out, axis, bit)
        upper = (me & bit) != 0
        out = jnp.concatenate([jnp.where(upper, other, out), jnp.where(upper, out, other)], axis=0)
        bit *= 2
    return out


def sum_small(v, axis):
    bit = 1
    while bit < lax.axis_size(axis):
        v = v + swap(v, axis, bit)
        bit *= 2
    return v


def gather_rows(own, axis):
    count = lax.axis_size(axis)
    lines = count // 2
    if lines > 4 or count % 2:
        return lax.all_gather(own, axis, axis=0, tiled=True)
    me = lax.axis_index(axis)
    z, y = me // 2, me % 2
    up, down = own, own
    below, above = {}, {}
    members = range(count)
    for j in range(1, lines):
        up = lax.ppermute(up, axis, [(s, s + 2) for s in members if s // 2 >= j - 1 and s + 2 < count])
        down = lax.ppermute(down, axis, [(s, s - 2) for s in members if s // 2 <= lines - j and s >= 2])
        below[j], above[j] = up, down
    out = jnp.zeros((count,) + own.shape, own.dtype)

    def place(out, v, line, side):
        return lax.dynamic_update_slice(out, v[None], (line * 2 + side, 0, 0))

    out = place(out, own, z, y)
    out = place(out, swap(own, axis), z, 1 - y)
    for j in range(1, lines):
        low, high = below[j], above[lines - j]
        low2 = lax.ppermute(low, axis, [(s, s ^ 1) for s in members if s // 2 >= j])
        high2 = lax.ppermute(high, axis, [(s, s ^ 1) for s in members if s // 2 + lines - j <= lines - 1])
        line = lax.rem(z + lines - j, lines)
        out = place(out, jnp.where(z >= j, low, high), line, y)
        out = place(out, jnp.where(z >= j, low2, high2), line, 1 - y)
    return out.reshape(count * own.shape[0], own.shape[1])


def scatter_rows(g, axis):
    count = lax.axis_size(axis)
    lines = count // 2
    if lines > 4 or count % 2:
        return lax.psum_scatter(g.astype(F32), axis, scatter_dimension=0, tiled=True)
    me = lax.axis_index(axis)
    z, y = me // 2, me % 2
    rows = g.shape[0] // count
    slots = g.reshape(lines, 2, rows, g.shape[1])
    members = range(count)

    def slot(j, side):
        return lax.dynamic_slice(
            slots, (lax.rem(z + j, lines), side, 0, 0), (1, 1, rows, g.shape[1]))[0, 0]

    part = {}
    for j in [lines - 1, *range(1, lines - 1), 0] if lines > 1 else [0]:
        got = swap(slot(j, 1 - y), axis)
        part[j] = slot(j, y).astype(F32) + got.astype(F32)
    up = down = None
    for d in range(lines - 1, 0, -1):
        to_up = part[d] if up is None else part[d] + up.astype(F32)
        to_down = part[lines - d] if down is None else part[lines - d] + down.astype(F32)
        up = lax.ppermute(
            to_up.astype(BF), axis, [(s, s + 2) for s in members if s // 2 + d <= lines - 1])
        down = lax.ppermute(
            to_down.astype(BF), axis, [(s, s - 2) for s in members if s // 2 >= d])
    out = part[0]
    if up is not None:
        out = out + up.astype(F32) + down.astype(F32)
    return out


def pair_order(first, mine, other, axis=0):
    return jnp.concatenate([jnp.where(first, mine, other), jnp.where(first, other, mine)], axis=axis)


def part_of(v, index, size, axis):
    return lax.dynamic_slice_in_dim(v, index * size, size, axis)


def scatter_product(factors, tensor_pos, ctx_pos, rows, cols):
    def block(row, col):
        total = None
        for left, right in factors:
            term = dot(part_of(left, row, rows, 0), part_of(right, col, cols, 0), 1, 1)
            total = term if total is None else total + term
        return total

    far_give = swap(block(1 - ctx_pos, 1 - tensor_pos).astype(BF), "tensor")
    far = block(1 - ctx_pos, tensor_pos) + far_give.astype(F32)
    crossed = swap(far.astype(BF), "ctx")
    near_give = swap(block(ctx_pos, 1 - tensor_pos).astype(BF), "tensor")
    near = block(ctx_pos, tensor_pos) + near_give.astype(F32)
    return near + crossed.astype(F32)


def pad_last(v, size):
    return jnp.pad(v, [(0, 0)] * (v.ndim - 1) + [(0, size - v.shape[-1])])


def per_device(tokens, segment_ids, norm_gain, w_z, w_x, w_bc, w_dt, conv_x, conv_x_bias, conv_bc,
               conv_bc_bias, a_log, dt_bias, d_skip, gate_gain, w_out, cotangent):
    shards = lax.axis_size("shard")
    ctx_count = lax.axis_size("ctx")
    tensor_count = lax.axis_size("tensor")
    assert ctx_count == 2 and tensor_count == 2
    shard_pos = lax.axis_index("shard")
    ctx_pos = lax.axis_index("ctx")
    tensor_pos = lax.axis_index("tensor")
    first_ctx, first_tensor = ctx_pos == 0, tensor_pos == 0
    piece, model = tokens.shape
    taps, group_heads, sub = conv_x.shape
    heads = group_heads // ctx_count
    width = sub * shards
    inner = heads * width
    inner_all = inner * ctx_count * tensor_count
    nstate = w_bc.shape[1] // 2
    count = piece * ctx_count
    out_cols = cotangent.shape[1]
    rows_w = w_x.shape[0]

    def own_heads(v, axis):
        return part_of(v, ctx_pos, v.shape[axis] // ctx_count, axis)

    half = piece // tensor_count
    sent = part_of(tokens, tensor_pos, half, 0)
    far_half = swap(sent, "ctx")

    wx_own, wz_own = own_heads(w_x, 1), own_heads(w_z, 1)
    wdt_own = pad_last(own_heads(w_dt, 1), LANES)
    wo_own = own_heads(w_out, 0).T
    pack = jnp.concatenate([wx_own, w_bc, wdt_own], axis=1)
    small = jnp.concatenate([
        norm_gain, own_heads(conv_x, 1).reshape(-1), own_heads(conv_x_bias, 0).reshape(-1),
        own_heads(gate_gain, 0).reshape(-1), conv_bc.reshape(-1), conv_bc_bias.reshape(-1)])
    small_rows = -(-small.shape[0] // (16 * LANES)) * 16
    small = jnp.pad(small, (0, small_rows * LANES - small.shape[0])).reshape(small_rows, LANES)
    smalls = gather_small(small, "shard").reshape(shards, -1).astype(F32)
    full_x = gather_rows(pack, "shard")
    full_z = gather_rows(wz_own, "shard")
    full_o = gather_rows(wo_own, "shard")

    far_other = swap(far_half, "tensor")
    far = pair_order(first_tensor, far_half, far_other)
    tokens_all = pair_order(first_ctx, tokens, far).astype(F32)

    at = 0

    def take(shape, axis):
        nonlocal at
        size = math.prod(shape)
        v = smalls[:, at : at + size].reshape((shards,) + shape)
        at += size
        return jnp.moveaxis(v, 0, axis).reshape(
            shape[:axis] + (shards * shape[axis],) + shape[axis + 1 :])

    full_norm = take((norm_gain.shape[0],), 0)
    taps_x = take((taps, heads, sub), 2).reshape(taps, inner)
    bias_x = take((heads, sub), 1).reshape(1, inner)
    gain = take((heads, sub), 1).reshape(1, inner)
    taps_bc = take((taps,) + conv_bc.shape[1:], 2).reshape(taps, 2 * nstate)
    bias_bc = take(conv_bc_bias.shape, 1).reshape(1, 2 * nstate)
    convp = jnp.concatenate([
        jnp.concatenate([taps_x, taps_bc], axis=1), jnp.concatenate([bias_x, bias_bc], axis=1),
        jnp.zeros((8 - taps - 1, inner + 2 * nstate), F32)], axis=0)
    alog_own, dtb_own, skip_own = own_heads(a_log, 0), own_heads(dt_bias, 0), own_heads(d_skip, 0)
    headp = jnp.concatenate([
        pad_last(jnp.stack([dtb_own, -jnp.exp(alog_own)]), LANES), jnp.zeros((6, LANES), F32)], axis=0)
    lanep = jnp.concatenate([jnp.repeat(skip_own, width)[None], gain, jnp.zeros((6, inner), F32)], axis=0)
    cols, rows = segment_tables(segment_ids[0], CHUNK)
    pick = head_pick(heads, width)

    rstd_in = lax.rsqrt(jnp.mean(tokens_all * tokens_all, axis=1, keepdims=True) + EPSILON)
    normed = (tokens_all * rstd_in * full_norm[None]).astype(BF)

    cot_far = swap(cotangent, "ctx")
    cot_side = pair_order(first_ctx, cotangent, cot_far)
    cot_all = pair_order(first_tensor, cot_side, swap(cot_side, "tensor"), axis=1)

    u = dot(normed, full_x, 1, 0)
    y, pre, h_in = ssd_forward(u, cols, rows, convp, headp, lanep, width)
    z = dot(normed, full_z, 1, 0)
    d_out = dot(cot_all, full_o, 1, 0)
    stats = gate_stats(y, z, d_out, lanep)
    stats = stats + swap(stats, "tensor")
    stats = stats + swap(stats, "ctx")
    gated, z16, dy, g_gain = gate_backward(y, z, d_out, stats, lanep, inner_all)
    branch = scatter_product([(gated, full_o)], tensor_pos, ctx_pos, piece, out_cols)
    own_tokens = part_of(tokens, tensor_pos, out_cols, 1).astype(F32)
    block_out = (own_tokens + branch).astype(BF)

    def weight_grad(left, right):
        return scatter_rows(dot(left, right, 0, 0).astype(BF), "shard")

    g_out = weight_grad(cot_all, gated)
    g_z = weight_grad(normed, z16)

    x16, dbc, dt16, g_conv, g_head, g_skip = ssd_backward(
        dy, y, u, pre, h_in, cols, rows, convp, headp, lanep, pick, width)
    side = tensor_pos * nstate
    dbc_give = swap(lax.dynamic_slice_in_dim(dbc, (1 - tensor_pos) * nstate, nstate, 1), "tensor")
    dbc_side = lax.dynamic_slice_in_dim(dbc, side, nstate, 1).astype(F32) + dbc_give.astype(F32)
    dbc_low = dbc_side.astype(BF)
    dbc_sum = dbc_low.astype(F32) + swap(dbc_low, "ctx").astype(F32)
    pre_side = lax.dynamic_slice_in_dim(pre, inner + side, nstate, 1)
    u_side = lax.dynamic_slice_in_dim(u, inner + side, nstate, 1)
    taps_side = lax.dynamic_slice_in_dim(taps_bc, side, nstate, 1)
    sig = sigmoid(pre_side)
    dpre = dbc_sum * sig * (1.0 + pre_side * (1.0 - sig))
    padded = jnp.concatenate([dpre, jnp.zeros((taps - 1, nstate), F32)], axis=0)
    du = taps_side[taps - 1 : taps] * dpre
    g_taps = [jnp.sum(dpre * u_side, axis=0)]
    for k in range(1, taps):
        moved = padded[k : k + count] * cols[:, 3 + k : 4 + k]
        du = du + taps_side[taps - 1 - k : taps - k] * moved
        g_taps.append(jnp.sum(moved * u_side, axis=0))
    g_bc_small = jnp.stack(g_taps[::-1] + [jnp.sum(dpre, axis=0)])
    owned = (lax.broadcasted_iota(jnp.int32, (count, 1), 0) // piece) == ctx_pos
    bcdt16 = jnp.concatenate([jnp.where(owned, du, 0.0).astype(BF), dt16], axis=1)

    g_x = weight_grad(normed, x16)
    g_bcdt = weight_grad(normed, bcdt16)

    w_bcdt = jnp.concatenate([
        lax.dynamic_slice_in_dim(full_x, inner + side, nstate, 1),
        full_x[:, inner + 2 * nstate :]], axis=1)
    d_normed = scatter_product(
        [(z16, full_z), (x16, full_x[:, :inner]), (bcdt16, w_bcdt)], tensor_pos, ctx_pos, piece, out_cols)
    rstd_own = part_of(rstd_in, ctx_pos, piece, 0)
    x_hat = own_tokens * rstd_own
    centered = d_normed * part_of(full_norm, tensor_pos, out_cols, 0)[None]
    row_sum = jnp.sum(centered * x_hat, axis=1)
    row_sum = row_sum + swap(row_sum, "tensor")
    d_tokens = rstd_own * (centered - x_hat * (row_sum / model)[:, None]) + cotangent.astype(F32)

    def both_ctx(g):
        low = g.astype(BF)
        return pair_order(first_ctx, low, swap(low, "ctx"), axis=1).astype(F32)

    grad_wz, grad_wx = both_ctx(g_z), both_ctx(g_x)
    grad_wout = both_ctx(g_out).T
    g_bc_part = g_bcdt[:, :nstate]
    g_bc_sum = g_bc_part + swap(g_bc_part, "ctx")
    grad_wbc = pair_order(first_tensor, g_bc_sum, swap(g_bc_sum, "tensor"), axis=1)
    g_dt = g_bcdt[:, nstate : nstate + heads]
    grad_wdt = pair_order(first_ctx, g_dt, swap(g_dt, "ctx"), axis=1)

    by_row = jnp.sum(wx_own.astype(F32) * g_x, axis=1) + jnp.sum(wz_own.astype(F32) * g_z, axis=1)
    by_row = by_row + jnp.sum(
        lax.dynamic_slice_in_dim(w_bc, side, nstate, 1).astype(F32) * g_bc_part, axis=1)
    by_row = by_row + jnp.sum(wdt_own[:, :heads].astype(F32) * g_dt, axis=1)
    by_row = sum_small(sum_small(by_row, "tensor"), "ctx")
    grad_norm = by_row / norm_gain.astype(F32)

    bundle = jnp.concatenate([
        g_conv[: taps + 1].reshape(-1), g_gain[0], g_bc_small.reshape(-1), g_head[:2].reshape(-1),
        pad_last(jnp.sum(g_skip[0].reshape(heads, width), axis=1), LANES)]).reshape(-1, LANES)
    bundle = sum_small(bundle, "shard").reshape(-1)
    lanes_part = bundle[: (taps + 2) * inner].reshape(taps + 2, heads, width)
    lanes_part = part_of(lanes_part, shard_pos, sub, 2)
    bc_small = bundle[(taps + 2) * inner : (taps + 2) * inner + (taps + 1) * nstate].reshape(taps + 1, nstate)
    bc_small = part_of(bc_small, shard_pos, nstate // shards, 1)
    head_part = bundle[(taps + 2) * inner + (taps + 1) * nstate :].reshape(3, LANES)[:, :heads]
    lanes_both = pair_order(first_ctx, lanes_part, swap(lanes_part, "ctx"), axis=1)
    head_both = pair_order(first_ctx, head_part, swap(head_part, "ctx"), axis=1)
    bc_both = pair_order(first_tensor, bc_small[:, None], swap(bc_small[:, None], "tensor"), axis=1)
    return (
        block_out, d_tokens, grad_norm, grad_wz, grad_wx, grad_wbc, grad_wdt,
        lanes_both[:taps], lanes_both[taps], bc_both[:taps], bc_both[taps],
        head_both[0], head_both[1], head_both[2], lanes_both[taps + 1], grad_wout,
    )


def solution(mesh):
    in_specs = (
        P(("shard", "ctx"), None),
        P("shard", None),
        P("shard"),
        P("shard", "tensor"),
        P("shard", "tensor"),
        P("shard", None),
        P("shard", "tensor"),
        P(None, "tensor", "shard"),
        P("tensor", "shard"),
        P(None, None, "shard"),
        P(None, "shard"),
        P("tensor"),
        P("tensor"),
        P("tensor"),
        P("tensor", "shard"),
        P("tensor", "shard"),
        P(("shard", "ctx"), "tensor"),
    )
    out_specs = (
        P(("shard", "ctx"), "tensor"),
        P(("shard", "ctx"), "tensor"),
        P("shard"),
        P("shard", "tensor"),
        P("shard", "tensor"),
        P("shard", None),
        P("shard", "tensor"),
        P(None, "tensor", "shard"),
        P("tensor", "shard"),
        P(None, None, "shard"),
        P(None, "shard"),
        P("tensor"),
        P("tensor"),
        P("tensor"),
        P("tensor", "shard"),
        P("tensor", "shard"),
    )
    return jax.shard_map(
        per_device, mesh=mesh, in_specs=in_specs, out_specs=out_specs, check_vma=False
    )
```
